128 devices in a mesh: row: 8 (over x, z_hi), col: 16 (over y, z_lo, core).
Axes of the slice: x: 4, y: 4, z: 4 (z_hi: 2, z_lo: 2; z = z_hi * 2 + z_lo), core: 2. Of those that a mesh axis runs over, the one named last changes fastest.
Arguments:
- grad_out: bfloat16 [16, 256, 8192], P('col', 'row'), may hold values from -0.25 to 0.25
- pre_act: bfloat16 [4096, 14336], P('col', 'row'), may hold values from -6 to 6
- down_weight: bfloat16 [8192, 14336], P('col', 'row'), may hold values from -3 to 3
Outputs:
- grad_pre: bfloat16 [4096, 14336], P('col', 'row')
- grad_weight: bfloat16 [8192, 14336], P('col', 'row')
The draws below stay inside these ranges and needn't reach their ends.
All inputs are finite; a program needn't handle non-finite values.
Results may differ from the reference program's by a relative error of at most 0.0048.
Values may be sent and summed in bfloat16 or wider, within the bound.
No kernel may reach another device: no remote copies, remote signals or barrier semaphores. Data moves between devices by JAX's collectives and lax.ppermute only.
A program may use at most 128 MiB of HBM per device.

```python
import math
import jax
import jax.numpy as jnp
from jax import lax

D = 8192
FFW = 14336
TOK_DEV = 32
TOKENS = 4096
N_ROW = 8
N_COL = 16


def shard_levels(own_key, dims, shards, low, top_value):
    def one(axis_at, blocks):
        steps = jax.random.uniform(jax.random.fold_in(jax.random.fold_in(own_key, 6), axis_at), (blocks,), jnp.float32, low / len(shards), top_value / len(shards))
        return jnp.repeat(jnp.exp(steps), dims[axis_at] // blocks).reshape((-1,) + (1,) * (len(dims) - axis_at - 1))

    level = one(*shards[0])
    for cut in shards[1:]:
        level = level * one(*cut)
    return level


def bell_draw(own_key, shape, width, limit, pieces=(), dtype=jnp.bfloat16):
    values = width * jax.random.normal(own_key, shape, jnp.float32)
    if pieces:
        values = values * shard_levels(own_key, shape, pieces, -0.22, 0.18)
    return jnp.clip(values, -limit, limit).astype(dtype)


def setup_inputs(seed: int = 0) -> dict:
    keys = jax.random.split(jax.random.key(seed), 4)
    grad_out = bell_draw(keys[0], (N_COL, TOK_DEV * N_ROW, D), (TOKENS ** -0.5), 0.25, ((0, 16), (1, 8)))
    pre_act = bell_draw(keys[1], (TOKENS, FFW), 1.5, 6.0, ((0, 16), (1, 8)))
    down_weight = bell_draw(keys[2], (D, FFW), (max(2 * D // TOKENS, 1)) ** -0.5, 3.0, ((0, 16), (1, 8)))
    return {"grad_out": grad_out, "pre_act": pre_act, "down_weight": down_weight}


def gelu_parts(pre_float):
    cumulative = 0.5 * (1.0 + jax.scipy.special.erf(pre_float / math.sqrt(2.0)))
    density = jnp.exp(-0.5 * pre_float * pre_float) / math.sqrt(2.0 * math.pi)
    return (pre_float * cumulative, cumulative + pre_float * density)

def reference(grad_out, pre_act, down_weight):
    grad_dy = grad_out.reshape(grad_out.shape[0] * grad_out.shape[1], grad_out.shape[2])
    activated, slope = gelu_parts(pre_act.astype(jnp.float32))
    hidden = activated.astype(jnp.bfloat16)
    grad_hidden = jnp.dot(grad_dy, down_weight, preferred_element_type=jnp.float32)
    grad_pre = (grad_hidden * slope).astype(jnp.bfloat16)
    grad_weight = lax.dot_general(grad_dy, hidden, (((0,), (0,)), ((), ())), preferred_element_type=jnp.float32)
    return (grad_pre, grad_weight.astype(jnp.bfloat16))
```

```python
import math

import jax
import jax.numpy as jnp
from jax import lax
from jax.sharding import Mesh, PartitionSpec as P

NAMES = ("x", "zh", "y", "zl", "core")
SIZES = {"x": 4, "zh": 2, "y": 4, "zl": 2, "core": 2}


def shift(value, axis, by):
    size = SIZES[axis]
    return lax.ppermute(value, axis, [(i, (i + by) % size) for i in range(size)])


def rolled(value, dim, axis):
    size = SIZES[axis]
    at = lax.axis_index(axis)
    if size == 2:
        return jnp.where(at == 0, value, jnp.flip(value, dim))
    return lax.dynamic_slice_in_dim(jnp.concatenate([value, value], dim), at, size, dim)


def unrolled(value, dim, axis):
    size = SIZES[axis]
    at = lax.axis_index(axis)
    if size == 2:
        return jnp.where(at == 0, value, jnp.flip(value, dim))
    return lax.dynamic_slice_in_dim(jnp.concatenate([value, value], dim), (size - at) % size, size, dim)


def gelu_parts(pre_float):
    cumulative = 0.5 * (1.0 + jax.scipy.special.erf(pre_float / math.sqrt(2.0)))
    density = jnp.exp(-0.5 * pre_float * pre_float) / math.sqrt(2.0 * math.pi)
    return (pre_float * cumulative, cumulative + pre_float * density)


def shards(grad_out, pre_act, weight):
    bf16, f32 = jnp.bfloat16, jnp.float32
    rows, width = grad_out.shape[1:]
    tokens, hidden_units = pre_act.shape
    own_rows = weight.shape[0]

    weight_other = shift(weight, "zl", 1)

    pieces = grad_out[0].reshape(rows, 4, 2, 2, own_rows)
    pieces = rolled(rolled(rolled(pieces, 1, "y"), 2, "zl"), 3, "core")
    pieces = pieces.transpose(3, 1, 0, 2, 4).reshape(2, 4, rows, 2 * own_rows)
    pieces = jnp.stack([pieces[0], shift(pieces[1], "core", 1)])
    grad = jnp.stack([pieces[:, 0]] + [shift(pieces[:, -s % 4], "y", -s) for s in (1, 2, 3)], 1)
    grad = jnp.stack([grad, shift(grad, "zh", 1)], 2)
    grad = jnp.stack([grad] + [shift(grad, "x", -s) for s in (1, 2, 3)], 2)
    grad = grad.reshape(8 * tokens, 2 * own_rows)

    pre = pre_act.astype(f32)
    activated, slope = gelu_parts(pre)
    hidden = activated.astype(bf16).reshape(4, 2, rows, hidden_units)
    hidden = rolled(rolled(hidden, 0, "x"), 1, "zh").reshape(tokens, hidden_units)
    hidden = jnp.stack([hidden] + [shift(hidden, "y", -s) for s in (1, 2, 3)])
    hidden = jnp.stack([hidden, shift(hidden, "core", 1)]).reshape(8 * tokens, hidden_units)

    weights = jnp.concatenate([weight, weight_other], 0)
    half = 4 * tokens
    partial_away = jnp.dot(grad[half:], weights, preferred_element_type=f32).astype(bf16)
    partial_away = shift(partial_away, "core", 1)
    partial = jnp.dot(grad[:half], weights, preferred_element_type=f32)
    partial = (partial + partial_away.astype(f32)).reshape(4, tokens, hidden_units)
    total = partial[0]
    for s in (1, 2, 3):
        total = total + shift(partial[s].astype(bf16), "y", s).astype(f32)
    total = unrolled(unrolled(total.reshape(4, 2, rows, hidden_units), 0, "x"), 1, "zh")
    grad_pre = (total.reshape(tokens, hidden_units) * slope).astype(bf16)

    contract = (((0,), (0,)), ((), ()))
    away = lax.dot_general(grad[:, own_rows:], hidden, contract, preferred_element_type=f32).astype(bf16)
    away = shift(away, "zl", 1)
    own = lax.dot_general(grad[:, :own_rows], hidden, contract, preferred_element_type=f32)
    return (grad_pre, (own + away.astype(f32)).astype(bf16))


def solution(mesh):
    sizes = tuple(SIZES[name] for name in NAMES)
    inner = Mesh(mesh.devices.reshape(sizes), NAMES)
    col, row = ("y", "zl", "core"), ("x", "zh")
    in_specs = (P(col, row, None), P(col, row), P(col, row))
    out_specs = (P(col, row), P(col, row))
    return jax.shard_map(shards, mesh=inner, in_specs=in_specs, out_specs=out_specs, check_vma=False)
```

```python
import functools
import math

import jax
import jax.numpy as jnp
from jax import lax
from jax.experimental import pallas as pl
from jax.experimental.pallas import tpu as pltpu
from jax.sharding import Mesh, PartitionSpec as P

NAMES = ("x", "zh", "y", "zl", "core")
SIZES = {"x": 4, "zh": 2, "y": 4, "zl": 2, "core": 2}
BF16, F32 = jnp.bfloat16, jnp.float32

STEP = {"b": lambda i: i ^ 1, "a": lambda i: 3 - i, "ab": lambda i: i ^ 2}


def swap(value, axis, step=None):
    move = STEP[step] if step else lambda i: 1 - i
    return lax.ppermute(value, axis, [(i, move(i)) for i in range(SIZES[axis])])


def around(axis):
    at = lax.axis_index(axis)
    return [at, at ^ 1, 3 - at, at ^ 2]


def after(value, *others):
    return lax.optimization_barrier((value,) + others)[0]


def gelu_parts(pre_float):
    cumulative = 0.5 * (1.0 + jax.scipy.special.erf(pre_float / math.sqrt(2.0)))
    density = jnp.exp(-0.5 * pre_float * pre_float) / math.sqrt(2.0 * math.pi)
    return (pre_float * cumulative, cumulative + pre_float * density)


def split_kernel(index, grad, near, away):
    size = near.shape[2] // 2
    for out, core in ((near, 0), (away, 1)):
        for y in range(4):
            for z in range(2):
                at = pl.multiple_of(index[core * 8 + y * 2 + z] * size, size)
                out[y, :, z * size : (z + 1) * size] = grad[:, pl.ds(at, size)]


def split_grad(grad, index):
    rows, width = grad.shape
    piece = jax.ShapeDtypeStruct((4, rows, width // 8), BF16)
    return pl.pallas_call(
        split_kernel,
        grid_spec=pltpu.PrefetchScalarGridSpec(
            num_scalar_prefetch=1,
            grid=(1,),
            in_specs=[pl.BlockSpec((rows, width), lambda i, s: (0, 0))],
            out_specs=[pl.BlockSpec(piece.shape, lambda i, s: (0, 0, 0))] * 2,
        ),
        out_shape=[piece, piece],
    )(index, grad)


def hidden_kernel(index, pre, left, right):
    value = gelu_parts(pre[...].astype(F32))[0].astype(BF16)
    half = value.shape[1] // 2
    left[...] = value[:, :half]
    right[...] = value[:, half:]


def make_hidden(pre, index):
    tokens, units = pre.shape
    rows, half = tokens // 8, units // 2
    out = jax.ShapeDtypeStruct((tokens, half), BF16)
    return pl.pallas_call(
        hidden_kernel,
        grid_spec=pltpu.PrefetchScalarGridSpec(
            num_scalar_prefetch=1,
            grid=(8,),
            in_specs=[pl.BlockSpec((rows, units), lambda i, s: (s[i], 0))],
            out_specs=[pl.BlockSpec((rows, half), lambda i, s: (i, 0))] * 2,
        ),
        out_shape=[out, out],
    )(index, pre)


def finish_kernel(index, pre, own_l, own_r, far_l, far_r, out):
    slope = gelu_parts(pre[...].astype(F32))[1]
    half = own_l.shape[1]
    out[:, :half] = ((own_l[...] + far_l[...].astype(F32)) * slope[:, :half]).astype(BF16)
    out[:, half:] = ((own_r[...] + far_r[...].astype(F32)) * slope[:, half:]).astype(BF16)


def finish(pre, own_l, own_r, far_l, far_r, index):
    tokens, units = pre.shape
    rows, half = tokens // 8, units // 2
    turned = pl.BlockSpec((rows, units), lambda i, s: (s[i], 0))
    plain = pl.BlockSpec((rows, half), lambda i, s: (i, 0))
    return pl.pallas_call(
        finish_kernel,
        grid_spec=pltpu.PrefetchScalarGridSpec(
            num_scalar_prefetch=1, grid=(8,), in_specs=[turned] + [plain] * 4, out_specs=turned
        ),
        out_shape=jax.ShapeDtypeStruct((tokens, units), BF16),
    )(index, pre, own_l, own_r, far_l, far_r)


def gather_square(first, second, axis):
    b1 = swap(first, axis, "b")
    a1 = swap(second, axis, "a")
    return b1, a1


def shards(grad_out, pre_act, weight):
    rows, width = grad_out.shape[1:]
    tokens, units = pre_act.shape
    half = units // 2
    own_rows = weight.shape[0]
    zl, core = lax.axis_index("zl"), lax.axis_index("core")
    grad_index = jnp.stack(
        [(y * 2 + (zl ^ z)) * 2 + (core ^ k) for k in range(2) for y in around("y") for z in range(2)]
    )
    zh = lax.axis_index("zh")
    token_index = jnp.stack([x * 2 + (zh ^ z) for x in around("x") for z in range(2)])

    near, away = split_grad(grad_out[0], grad_index)
    sibling = swap(away, "core")
    weight_l, weight_r = weight[:, :half], weight[:, half:]
    other_l = swap(weight_l, "zl")
    hidden_l, hidden_r = make_hidden(after(pre_act, away), token_index)

    both = jnp.stack([near, sibling])
    grad = jnp.stack([both[:, 0]] + [swap(both[:, s], "y", m) for s, m in ((1, "b"), (2, "a"), (3, "ab"))], 1)
    grad = grad.reshape(8, rows, 2 * own_rows)
    grad_far = swap(grad, "zh")

    def gather_x(piece):
        mine, theirs = piece[..., own_rows:], piece[..., :own_rows]
        mine_b = swap(mine, "x", "b")
        theirs_a = swap(theirs, "x", "a")
        mine = jnp.stack([mine, mine_b])
        theirs = jnp.stack([theirs, theirs_a])
        mine_a = swap(mine, "x", "a")
        theirs_b = swap(theirs, "x", "b")
        return [mine[0], mine[1], mine_a[0], mine_a[1]], [theirs[0], theirs_b[0], theirs[1], theirs_b[1]]

    hidden_lb = swap(after(hidden_l, grad), "y", "b")
    hidden_ra = swap(after(hidden_r, grad), "y", "a")
    near_o, near_t = gather_x(grad)
    other_r = swap(after(weight_r, grad_far), "zl")
    hidden_l = jnp.stack([hidden_l, hidden_lb])
    hidden_r = jnp.stack([hidden_r, hidden_ra])
    hidden_la = swap(hidden_l, "y", "a")
    hidden_rb = swap(hidden_r, "y", "b")
    far_o, far_t = gather_x(after(grad_far, near_o[3]))
    hidden_l = jnp.concatenate([hidden_l, hidden_la])
    hidden_r = jnp.stack([hidden_r[0], hidden_rb[0], hidden_r[1], hidden_rb[1]])
    hidden_l = jnp.concatenate([hidden_l, swap(hidden_l, "core")]).reshape(8 * tokens, half)
    hidden_r = jnp.concatenate([hidden_r, swap(hidden_r, "core")]).reshape(8 * tokens, half)

    def together(near, far):
        return jnp.stack([v for pair in zip(near, far) for v in pair], 1).reshape(8 * tokens, own_rows)

    grad_other, grad_own = together(near_o, far_o), together(near_t, far_t)
    grad_other, grad_own, hidden_l, hidden_r, other_l, other_r = lax.optimization_barrier(
        (grad_other, grad_own, hidden_l, hidden_r, other_l, other_r)
    )

    def outer(g, h):
        return lax.dot_general(g, h, (((0,), (0,)), ((), ())), preferred_element_type=F32)

    sent_l = outer(grad_other, hidden_l).astype(BF16)
    sent_r = outer(grad_other, hidden_r).astype(BF16)
    got_l = swap(sent_l, "zl")
    got_r = swap(sent_r, "zl")

    grad_both = after(jnp.concatenate([grad_own, grad_other], 1), sent_r)
    w_l = jnp.concatenate([weight_l, other_l])
    w_r = jnp.concatenate([weight_r, other_r])
    edge = 4 * tokens
    away_l = jnp.dot(grad_both[edge:], w_l, preferred_element_type=F32).astype(BF16)
    away_l = swap(away_l, "core")
    away_r = jnp.dot(grad_both[edge:], w_r, preferred_element_type=F32).astype(BF16)
    away_r = swap(away_r, "core")
    part_l = jnp.dot(grad_both[:edge], w_l, preferred_element_type=F32) + away_l.astype(F32)
    part_r = jnp.dot(grad_both[:edge], w_r, preferred_element_type=F32) + away_r.astype(F32)
    part_l = part_l.reshape(2, 2, tokens, half)
    part_r = part_r.reshape(2, 2, tokens, half)
    part_l = part_l[0] + swap(part_l[1].astype(BF16), "y", "a").astype(F32)
    part_r = part_r[:, 0] + swap(part_r[:, 1].astype(BF16), "y", "b").astype(F32)
    far_l = swap(part_l[1].astype(BF16), "y", "b")
    far_r = swap(part_r[1].astype(BF16), "y", "a")
    grad_pre = finish(pre_act, part_l[0], part_r[0], far_l, far_r, token_index)

    kept_l = outer(grad_own, hidden_l) + got_l.astype(F32)
    kept_r = outer(grad_own, hidden_r) + got_r.astype(F32)
    return (grad_pre, jnp.concatenate([kept_l, kept_r], 1).astype(BF16))


def solution(mesh):
    sizes = tuple(SIZES[name] for name in NAMES)
    inner = Mesh(mesh.devices.reshape(sizes), NAMES)
    col, row = ("y", "zl", "core"), ("x", "zh")
    in_specs = (P(col, row, None), P(col, row), P(col, row))
    out_specs = (P(col, row), P(col, row))
    return jax.shard_map(shards, mesh=inner, in_specs=in_specs, out_specs=out_specs, check_vma=False)
```

```python
import functools
import math

import jax
import jax.numpy as jnp
from jax import lax
from jax.experimental import pallas as pl
from jax.experimental.pallas import tpu as pltpu
from jax.sharding import Mesh, PartitionSpec as P

NAMES = ("x", "zh", "y", "zl", "core")
SIZES = {"x": 4, "zh": 2, "y": 4, "zl": 2, "core": 2}
BF16, F32 = jnp.bfloat16, jnp.float32
VMEM = pl.BlockSpec(memory_space=pltpu.VMEM)

STEP = {"b": lambda i: i ^ 1, "a": lambda i: 3 - i, "ab": lambda i: i ^ 2}


def swap(value, axis, step=None):
    move = STEP[step] if step else lambda i: 1 - i
    return lax.ppermute(value, axis, [(i, move(i)) for i in range(SIZES[axis])])


def around(axis):
    at = lax.axis_index(axis)
    return [at, at ^ 1, 3 - at, at ^ 2]


def after(value, *others):
    return lax.optimization_barrier((value,) + others)[0]


def gelu_parts(pre_float):
    cumulative = 0.5 * (1.0 + jax.scipy.special.erf(pre_float / math.sqrt(2.0)))
    density = jnp.exp(-0.5 * pre_float * pre_float) / math.sqrt(2.0 * math.pi)
    return (pre_float * cumulative, cumulative + pre_float * density)


def split_kernel(grad, near, away):
    size = near.shape[2] // 2
    zl, core = lax.axis_index("zl"), lax.axis_index("core")
    for out, k in ((near, core), (away, 1 - core)):
        for n, y in enumerate(around("y")):
            for z, other in enumerate((zl, 1 - zl)):
                at = pl.multiple_of(((y * 2 + other) * 2 + k) * size, size)
                out[n, :, z * size : (z + 1) * size] = grad[:, pl.ds(at, size)]


def split_grad(grad):
    rows, width = grad.shape
    piece = jax.ShapeDtypeStruct((4, rows, width // 8), BF16)
    return pl.pallas_call(split_kernel, in_specs=[VMEM], out_specs=[VMEM] * 2, out_shape=[piece, piece])(grad)


def token_blocks(rows):
    zh = lax.axis_index("zh")
    return [pl.multiple_of((x * 2 + z) * rows, rows) for x in around("x") for z in (zh, 1 - zh)]


def hidden_kernel(pre, left, right, slope_l, slope_r):
    rows, half = pre.shape[0] // 8, pre.shape[1] // 2
    for n, at in enumerate(token_blocks(rows)):
        value, slope = gelu_parts(pre[pl.ds(at, rows), :].astype(F32))
        here = pl.ds(n * rows, rows)
        left[here, :] = value[:, :half].astype(BF16)
        right[here, :] = value[:, half:].astype(BF16)
        slope_l[here, :] = slope[:, :half]
        slope_r[here, :] = slope[:, half:]


def make_hidden(pre):
    tokens, units = pre.shape
    out = [jax.ShapeDtypeStruct((tokens, units // 2), t) for t in (BF16, BF16, F32, F32)]
    return pl.pallas_call(hidden_kernel, in_specs=[VMEM], out_specs=[VMEM] * 4, out_shape=out)(pre)


def finish_kernel(slope_l, slope_r, own_l, own_r, far_l, far_r, out):
    rows, half = out.shape[0] // 8, out.shape[1] // 2
    for n, at in enumerate(token_blocks(rows)):
        here = pl.ds(n * rows, rows)
        left = (own_l[here, :] + far_l[here, :].astype(F32)) * slope_l[here, :]
        right = (own_r[here, :] + far_r[here, :].astype(F32)) * slope_r[here, :]
        out[pl.ds(at, rows), :half] = left.astype(BF16)
        out[pl.ds(at, rows), half:] = right.astype(BF16)


def finish(*args):
    tokens, half = args[0].shape
    out = jax.ShapeDtypeStruct((tokens, 2 * half), BF16)
    return pl.pallas_call(finish_kernel, in_specs=[VMEM] * 6, out_specs=VMEM, out_shape=out)(*args)


def outer(g, h):
    return lax.dot_general(g, h, (((0,), (0,)), ((), ())), preferred_element_type=F32)


def inner(g, w):
    return jnp.dot(g, w, preferred_element_type=F32)


def shards(grad_out, pre_act, weight):
    rows, width = grad_out.shape[1:]
    tokens, units = pre_act.shape
    half = units // 2
    own_rows = weight.shape[0]

    near, away = split_grad(grad_out[0])
    sibling = swap(away, "core")
    weight_l, weight_r = weight[:, :half], weight[:, half:]
    other_l = swap(weight_l, "zl")
    hidden_l, hidden_r, slope_l, slope_r = make_hidden(after(pre_act, near))

    both = jnp.stack([near, after(sibling, hidden_l)])
    grad = jnp.stack([both[:, 0]] + [swap(both[:, s], "y", m) for s, m in ((1, "b"), (2, "a"), (3, "ab"))], 1)
    grad = grad.reshape(8, rows, 2 * own_rows)

    near_o, near_t = grad[..., own_rows:], grad[..., :own_rows]
    near_ob, near_ta = swap(near_o, "x", "b"), swap(near_t, "x", "a")
    hidden_l, hidden_r = after(hidden_l, grad), after(hidden_r, grad)
    hidden_lb, hidden_ra = swap(hidden_l, "y", "b"), swap(hidden_r, "y", "a")
    near_ob, near_ta, hidden_lb, hidden_ra, other_l, grad = lax.optimization_barrier(
        (near_ob, near_ta, hidden_lb, hidden_ra, other_l, grad)
    )
    near_o, near_t = jnp.stack([near_o, near_ob]), jnp.stack([near_t, near_ta])
    hidden_l, hidden_r = jnp.stack([hidden_l, hidden_lb]), jnp.stack([hidden_r, hidden_ra])
    grad_far = swap(grad, "zh")
    near_oa, near_tb = swap(near_o, "x", "a"), swap(near_t, "x", "b")
    hidden_la, hidden_rb = swap(hidden_l, "y", "a"), swap(hidden_r, "y", "b")
    near_oa, near_tb, grad_far = lax.optimization_barrier((near_oa, near_tb, grad_far))
    far_o, far_t = grad_far[..., own_rows:], grad_far[..., :own_rows]
    far_ob, far_ta = swap(far_o, "x", "b"), swap(far_t, "x", "a")
    other_r = swap(after(weight_r, grad_far), "zl")
    far_ob, far_ta, hidden_la, hidden_rb = lax.optimization_barrier((far_ob, far_ta, hidden_la, hidden_rb))
    far_o, far_t = jnp.stack([far_o, far_ob]), jnp.stack([far_t, far_ta])
    far_oa, far_tb = swap(far_o, "x", "a"), swap(far_t, "x", "b")
    hidden_l = jnp.concatenate([hidden_l, hidden_la])
    hidden_r = jnp.stack([hidden_r[0], hidden_rb[0], hidden_r[1], hidden_rb[1]])
    hidden_l = jnp.concatenate([hidden_l, swap(hidden_l, "core")]).reshape(8 * tokens, half)
    hidden_r = jnp.concatenate([hidden_r, swap(hidden_r, "core")]).reshape(8 * tokens, half)

    grad_o = [near_o[0], far_o[0], near_o[1], far_o[1], near_oa[0], far_oa[0], near_oa[1], far_oa[1]]
    grad_t = [near_t[0], far_t[0], near_tb[0], far_tb[0], near_t[1], far_t[1], near_tb[1], far_tb[1]]
    grad_other = jnp.stack(grad_o, 1).reshape(8 * tokens, own_rows)
    grad_own = jnp.stack(grad_t, 1).reshape(8 * tokens, own_rows)
    grad_other, grad_own, hidden_l, hidden_r, other_l, other_r = lax.optimization_barrier(
        (grad_other, grad_own, hidden_l, hidden_r, other_l, other_r)
    )

    grad_both = jnp.concatenate([grad_own, grad_other], 1)
    w_l = jnp.concatenate([weight_l, other_l])
    w_r = jnp.concatenate([weight_r, other_r])
    edge = 4 * tokens
    away_l = inner(grad_both[edge:], w_l).astype(BF16)
    away_r = inner(after(grad_both, away_l)[edge:], w_r).astype(BF16)
    sent_l = outer(after(grad_other, away_r), hidden_l).astype(BF16)
    sent_r = outer(after(grad_other, sent_l), hidden_r).astype(BF16)
    got_l, got_r = swap(sent_l, "zl"), swap(sent_r, "zl")
    back_l, back_r = swap(away_l, "core"), swap(away_r, "core")
    back_l = after(back_l, sent_r)
    part_l = inner(grad_both[:edge], w_l) + back_l.astype(F32)
    back_r = after(back_r, part_l)
    part_r = inner(grad_both[:edge], w_r) + back_r.astype(F32)
    part_l = part_l.reshape(2, 2, tokens, half)
    part_r = part_r.reshape(2, 2, tokens, half)
    next_l, next_r = swap(part_l[1].astype(BF16), "y", "a"), swap(part_r[:, 1].astype(BF16), "y", "b")
    kept_l = outer(after(grad_own, part_r), hidden_l)
    kept_r = outer(after(grad_own, kept_l), hidden_r)
    next_l, next_r, kept_l, kept_r = lax.optimization_barrier((next_l, next_r, kept_l, kept_r))
    part_l = part_l[0] + next_l.astype(F32)
    part_r = part_r[:, 0] + next_r.astype(F32)
    far_l, far_r = swap(part_l[1].astype(BF16), "y", "b"), swap(part_r[1].astype(BF16), "y", "a")
    grad_pre = finish(slope_l, slope_r, part_l[0], part_r[0], far_l, far_r)
    kept = jnp.concatenate([kept_l + got_l.astype(F32), kept_r + got_r.astype(F32)], 1)
    return (grad_pre, kept.astype(BF16))


def solution(mesh):
    sizes = tuple(SIZES[name] for name in NAMES)
    inner_mesh = Mesh(mesh.devices.reshape(sizes), NAMES)
    col, row = ("y", "zl", "core"), ("x", "zh")
    in_specs = (P(col, row, None), P(col, row), P(col, row))
    out_specs = (P(col, row), P(col, row))
    return jax.shard_map(shards, mesh=inner_mesh, in_specs=in_specs, out_specs=out_specs, check_vma=False)
```

```python
import functools
import math

import jax
import jax.numpy as jnp
from jax import lax
from jax.experimental import pallas as pl
from jax.experimental.pallas import tpu as pltpu
from jax.sharding import Mesh, PartitionSpec as P

NAMES = ("x", "zh", "y", "zl", "core")
SIZES = {"x": 4, "zh": 2, "y": 4, "zl": 2, "core": 2}
BF16, F32 = jnp.bfloat16, jnp.float32
VMEM = pl.BlockSpec(memory_space=pltpu.VMEM)
SMALL = pltpu.CompilerParams(vmem_limit_bytes=16 * 1024 * 1024)

STEP = {"b": lambda i: i ^ 1, "a": lambda i: 3 - i, "ab": lambda i: i ^ 2}


def swap(value, axis, step=None):
    move = STEP[step] if step else lambda i: 1 - i
    return lax.ppermute(value, axis, [(i, move(i)) for i in range(SIZES[axis])])


def around(axis):
    at = lax.axis_index(axis)
    return [at, at ^ 1, 3 - at, at ^ 2]


def after(value, *others):
    return lax.optimization_barrier((value,) + others)[0]


def gelu_parts(pre_float):
    cumulative = 0.5 * (1.0 + jax.scipy.special.erf(pre_float / math.sqrt(2.0)))
    density = jnp.exp(-0.5 * pre_float * pre_float) / math.sqrt(2.0 * math.pi)
    return (pre_float * cumulative, cumulative + pre_float * density)


def split_kernel(grad, near, away):
    size = near.shape[2] // 2
    zl, core = lax.axis_index("zl"), lax.axis_index("core")
    for out, k in ((near, core), (away, 1 - core)):
        for n, y in enumerate(around("y")):
            for z, other in enumerate((zl, 1 - zl)):
                at = pl.multiple_of(((y * 2 + other) * 2 + k) * size, size)
                out[n, :, z * size : (z + 1) * size] = grad[:, pl.ds(at, size)]


def split_grad(grad):
    rows, width = grad.shape
    piece = jax.ShapeDtypeStruct((4, rows, width // 8), BF16)
    return pl.pallas_call(split_kernel, in_specs=[VMEM], out_specs=[VMEM] * 2, out_shape=[piece, piece], compiler_params=SMALL)(grad)


def token_blocks(rows):
    zh = lax.axis_index("zh")
    return [pl.multiple_of((x * 2 + z) * rows, rows) for x in around("x") for z in (zh, 1 - zh)]


def hidden_kernel(pre, left, right, slope_l, slope_r):
    rows, half = pre.shape[0] // 8, pre.shape[1] // 2
    for n, at in enumerate(token_blocks(rows)):
        value, slope = gelu_parts(pre[pl.ds(at, rows), :].astype(F32))
        here = pl.ds(n * rows, rows)
        left[here, :] = value[:, :half].astype(BF16)
        right[here, :] = value[:, half:].astype(BF16)
        slope_l[here, :] = slope[:, :half]
        slope_r[here, :] = slope[:, half:]


def make_hidden(pre):
    tokens, units = pre.shape
    out = [jax.ShapeDtypeStruct((tokens, units // 2), t) for t in (BF16, BF16, F32, F32)]
    return pl.pallas_call(hidden_kernel, in_specs=[VMEM], out_specs=[VMEM] * 4, out_shape=out, compiler_params=SMALL)(pre)


def finish_kernel(slope_l, slope_r, own_l, own_r, far_l, far_r, out):
    rows, half = out.shape[0] // 8, out.shape[1] // 2
    for n, at in enumerate(token_blocks(rows)):
        here = pl.ds(n * rows, rows)
        left = (own_l[here, :] + far_l[here, :].astype(F32)) * slope_l[here, :]
        right = (own_r[here, :] + far_r[here, :].astype(F32)) * slope_r[here, :]
        out[pl.ds(at, rows), :half] = left.astype(BF16)
        out[pl.ds(at, rows), half:] = right.astype(BF16)


def finish(*args):
    tokens, half = args[0].shape
    out = jax.ShapeDtypeStruct((tokens, 2 * half), BF16)
    return pl.pallas_call(finish_kernel, in_specs=[VMEM] * 6, out_specs=VMEM, out_shape=out, compiler_params=SMALL)(*args)


def outer(g, h):
    return lax.dot_general(g, h, (((0,), (0,)), ((), ())), preferred_element_type=F32)


def inner(g, w):
    return jnp.dot(g, w, preferred_element_type=F32)


def shards(grad_out, pre_act, weight):
    rows, width = grad_out.shape[1:]
    tokens, units = pre_act.shape
    half = units // 2
    own_rows = weight.shape[0]

    near, away = split_grad(grad_out[0])
    sibling = swap(away, "core")
    weight_l, weight_r = weight[:, :half], weight[:, half:]
    other_l = swap(weight_l, "zl")

    both = jnp.stack([near, after(sibling, weight_l)])
    hidden_l, hidden_r, slope_l, slope_r = make_hidden(after(pre_act, both))
    grad = jnp.stack([both[:, 0]] + [swap(both[:, s], "y", m) for s, m in ((1, "b"), (2, "a"), (3, "ab"))], 1)
    grad = grad.reshape(8, rows, 2 * own_rows)

    near_o, near_t = grad[..., own_rows:], grad[..., :own_rows]
    near_ob, near_ta = swap(near_o, "x", "b"), swap(near_t, "x", "a")
    hidden_l, hidden_r = after(hidden_l, grad), after(hidden_r, grad)
    hidden_lb, hidden_ra = swap(hidden_l, "y", "b"), swap(hidden_r, "y", "a")
    near_ob, near_ta, hidden_lb, hidden_ra, other_l, grad = lax.optimization_barrier(
        (near_ob, near_ta, hidden_lb, hidden_ra, other_l, grad)
    )
    near_o, near_t = jnp.stack([near_o, near_ob]), jnp.stack([near_t, near_ta])
    hidden_l, hidden_r = jnp.stack([hidden_l, hidden_lb]), jnp.stack([hidden_r, hidden_ra])
    grad_far = swap(grad, "zh")
    near_oa, near_tb = swap(near_o, "x", "a"), swap(near_t, "x", "b")
    hidden_la, hidden_rb = swap(hidden_l, "y", "a"), swap(hidden_r, "y", "b")
    near_oa, near_tb, grad_far = lax.optimization_barrier((near_oa, near_tb, grad_far))
    far_o, far_t = grad_far[..., own_rows:], grad_far[..., :own_rows]
    far_ob, far_ta = swap(far_o, "x", "b"), swap(far_t, "x", "a")
    other_r = swap(after(weight_r, grad_far), "zl")
    far_ob, far_ta = lax.optimization_barrier((far_ob, far_ta))
    far_o, far_t = jnp.stack([far_o, far_ob]), jnp.stack([far_t, far_ta])
    far_oa, far_tb = swap(far_o, "x", "a"), swap(far_t, "x", "b")
    hidden_l = jnp.concatenate([hidden_l, hidden_la])
    hidden_r = jnp.stack([hidden_r[0], hidden_rb[0], hidden_r[1], hidden_rb[1]])
    hidden_l = jnp.concatenate([hidden_l, swap(hidden_l, "core")]).reshape(8 * tokens, half)
    hidden_r = jnp.concatenate([hidden_r, swap(hidden_r, "core")]).reshape(8 * tokens, half)

    grad_o = [near_o[0], far_o[0], near_o[1], far_o[1], near_oa[0], far_oa[0], near_oa[1], far_oa[1]]
    grad_t = [near_t[0], far_t[0], near_tb[0], far_tb[0], near_t[1], far_t[1], near_tb[1], far_tb[1]]
    grad_other = jnp.stack(grad_o, 1).reshape(8 * tokens, own_rows)
    grad_own = jnp.stack(grad_t, 1).reshape(8 * tokens, own_rows)
    grad_other, grad_own, hidden_l, hidden_r, other_l, other_r = lax.optimization_barrier(
        (grad_other, grad_own, hidden_l, hidden_r, other_l, other_r)
    )

    grad_both = jnp.concatenate([grad_own, grad_other], 1)
    w_l = jnp.concatenate([weight_l, other_l])
    w_r = jnp.concatenate([weight_r, other_r])
    edge = 4 * tokens
    sent_l = outer(grad_other, hidden_l).astype(BF16)
    got_l = swap(sent_l, "zl")
    away_l = inner(after(grad_both, sent_l)[edge:], w_l).astype(BF16)
    away_r = inner(after(grad_both, away_l)[edge:], w_r).astype(BF16)
    back_l, back_r = swap(away_l, "core"), swap(away_r, "core")
    sent_r = outer(after(grad_other, away_r), hidden_r).astype(BF16)
    got_r = swap(sent_r, "zl")
    back_l = after(back_l, sent_r)
    part_l = inner(grad_both[:edge], w_l) + back_l.astype(F32)
    part_l = part_l.reshape(2, 2, tokens, half)
    next_l = swap(part_l[1].astype(BF16), "y", "a")
    back_r = after(back_r, part_l)
    part_r = inner(grad_both[:edge], w_r) + back_r.astype(F32)
    part_r = part_r.reshape(2, 2, tokens, half)
    next_r = swap(part_r[:, 1].astype(BF16), "y", "b")
    kept_l = outer(after(grad_own, part_r), hidden_l)
    kept_r = outer(after(grad_own, kept_l), hidden_r)
    next_l, next_r, kept_l, kept_r = lax.optimization_barrier((next_l, next_r, kept_l, kept_r))
    far_l = swap((part_l[0, 1] + next_l[1].astype(F32)).astype(BF16), "y", "b")
    far_r = swap((part_r[1, 0] + next_r[1].astype(F32)).astype(BF16), "y", "a")
    own_l = part_l[0, 0] + next_l[0].astype(F32)
    own_r = part_r[0, 0] + next_r[0].astype(F32)
    grad_pre = finish(slope_l, slope_r, own_l, own_r, far_l, far_r)
    kept_l = (kept_l + after(got_l, own_l, own_r).astype(F32)).astype(BF16)
    kept_r = (kept_r + after(got_r, grad_pre).astype(F32)).astype(BF16)
    return (grad_pre, jnp.concatenate([kept_l, kept_r], 1))


def solution(mesh):
    sizes = tuple(SIZES[name] for name in NAMES)
    inner_mesh = Mesh(mesh.devices.reshape(sizes), NAMES)
    col, row = ("y", "zl", "core"), ("x", "zh")
    in_specs = (P(col, row, None), P(col, row), P(col, row))
    out_specs = (P(col, row), P(col, row))
    return jax.shard_map(shards, mesh=inner_mesh, in_specs=in_specs, out_specs=out_specs, check_vma=False)
```

```python
import functools
import math

import jax
import jax.numpy as jnp
from jax import lax
from jax.experimental import pallas as pl
from jax.experimental.pallas import tpu as pltpu
from jax.sharding import Mesh, PartitionSpec as P

NAMES = ("x", "zh", "y", "zl", "core")
SIZES = {"x": 4, "zh": 2, "y": 4, "zl": 2, "core": 2}
BF16, F32 = jnp.bfloat16, jnp.float32
VMEM = pl.BlockSpec(memory_space=pltpu.VMEM)
SMALL = pltpu.CompilerParams(vmem_limit_bytes=16 * 1024 * 1024)

STEP = {"b": lambda i: i ^ 1, "a": lambda i: 3 - i, "ab": lambda i: i ^ 2}


def swap(value, axis, step=None):
    move = STEP[step] if step else lambda i: 1 - i
    return lax.ppermute(value, axis, [(i, move(i)) for i in range(SIZES[axis])])


def around(axis):
    at = lax.axis_index(axis)
    return [at, at ^ 1, 3 - at, at ^ 2]


def after(value, *others):
    return lax.optimization_barrier((value,) + others)[0]


def gelu_parts(pre_float):
    cumulative = 0.5 * (1.0 + jax.scipy.special.erf(pre_float / math.sqrt(2.0)))
    density = jnp.exp(-0.5 * pre_float * pre_float) / math.sqrt(2.0 * math.pi)
    return (pre_float * cumulative, cumulative + pre_float * density)


def split_kernel(grad, near, away):
    size = near.shape[2] // 2
    zl, core = lax.axis_index("zl"), lax.axis_index("core")
    for out, k in ((near, core), (away, 1 - core)):
        for n, y in enumerate(around("y")):
            for z, other in enumerate((zl, 1 - zl)):
                at = pl.multiple_of(((y * 2 + other) * 2 + k) * size, size)
                out[n, :, z * size : (z + 1) * size] = grad[:, pl.ds(at, size)]


def split_grad(grad):
    rows, width = grad.shape
    piece = jax.ShapeDtypeStruct((4, rows, width // 8), BF16)
    return pl.pallas_call(split_kernel, in_specs=[VMEM], out_specs=[VMEM] * 2, out_shape=[piece, piece], compiler_params=SMALL)(grad)


def token_blocks(rows):
    zh = lax.axis_index("zh")
    return [pl.multiple_of((x * 2 + z) * rows, rows) for x in around("x") for z in (zh, 1 - zh)]


def hidden_kernel(pre, left, right, slope_l, slope_r):
    rows, half = pre.shape[0] // 8, pre.shape[1] // 2
    for n, at in enumerate(token_blocks(rows)):
        value, slope = gelu_parts(pre[pl.ds(at, rows), :].astype(F32))
        here = pl.ds(n * rows, rows)
        left[here, :] = value[:, :half].astype(BF16)
        right[here, :] = value[:, half:].astype(BF16)
        slope_l[here, :] = slope[:, :half]
        slope_r[here, :] = slope[:, half:]


def make_hidden(pre):
    tokens, units = pre.shape
    out = [jax.ShapeDtypeStruct((tokens, units // 2), t) for t in (BF16, BF16, F32, F32)]
    return pl.pallas_call(hidden_kernel, in_specs=[VMEM], out_specs=[VMEM] * 4, out_shape=out, compiler_params=SMALL)(pre)


def finish_kernel(slope_l, slope_r, own_l, own_r, far_l, far_r, out):
    rows, half = out.shape[0] // 8, out.shape[1] // 2
    for n, at in enumerate(token_blocks(rows)):
        here = pl.ds(n * rows, rows)
        left = (own_l[here, :] + far_l[here, :].astype(F32)) * slope_l[here, :]
        right = (own_r[here, :] + far_r[here, :].astype(F32)) * slope_r[here, :]
        out[pl.ds(at, rows), :half] = left.astype(BF16)
        out[pl.ds(at, rows), half:] = right.astype(BF16)


def finish(*args):
    tokens, half = args[0].shape
    out = jax.ShapeDtypeStruct((tokens, 2 * half), BF16)
    return pl.pallas_call(finish_kernel, in_specs=[VMEM] * 6, out_specs=VMEM, out_shape=out, compiler_params=SMALL)(*args)


def outer(g, h):
    return lax.dot_general(g, h, (((0,), (0,)), ((), ())), preferred_element_type=F32)


def inner(g, w):
    return jnp.dot(g, w, preferred_element_type=F32)


def shards(grad_out, pre_act, weight):
    rows, width = grad_out.shape[1:]
    tokens, units = pre_act.shape
    half = units // 2
    own_rows = weight.shape[0]

    near, away = split_grad(grad_out[0])
    sibling = swap(away, "core")
    cut = own_rows * 5 // 16
    other_top = swap(weight[:cut], "zl")

    both = jnp.stack([near, sibling])
    hidden_l, hidden_r, slope_l, slope_r = make_hidden(after(pre_act, both))
    grad = jnp.stack([both[:, 0]] + [swap(both[:, s], "y", m) for s, m in ((1, "b"), (2, "a"), (3, "ab"))], 1)
    grad = grad.reshape(8, rows, 2 * own_rows)

    near_o, near_t = grad[..., own_rows:], grad[..., :own_rows]
    near_ob, near_ta = swap(near_o, "x", "b"), swap(near_t, "x", "a")
    grad_far = swap(after(grad, other_top), "zh")
    hidden_l, hidden_r = after(hidden_l, grad), after(hidden_r, grad)
    hidden_lb, hidden_ra = swap(hidden_l, "y", "b"), swap(hidden_r, "y", "a")
    near_ob, near_ta = lax.optimization_barrier((near_ob, near_ta))
    near_o, near_t = jnp.stack([near_o, near_ob]), jnp.stack([near_t, near_ta])
    near_oa, near_tb = swap(near_o, "x", "a"), swap(near_t, "x", "b")
    hidden_l, hidden_r = jnp.stack([hidden_l, hidden_lb]), jnp.stack([hidden_r, hidden_ra])
    hidden_la, hidden_rb = swap(hidden_l, "y", "a"), swap(hidden_r, "y", "b")
    other_low = swap(after(weight[cut:], grad_far), "zl")
    near_oa, near_tb, grad_far = lax.optimization_barrier((near_oa, near_tb, grad_far))
    far_o, far_t = grad_far[..., own_rows:], grad_far[..., :own_rows]
    far_ob, far_ta = swap(far_o, "x", "b"), swap(far_t, "x", "a")
    far_ob, far_ta = lax.optimization_barrier((far_ob, far_ta))
    far_o, far_t = jnp.stack([far_o, far_ob]), jnp.stack([far_t, far_ta])
    far_oa, far_tb = swap(far_o, "x", "a"), swap(far_t, "x", "b")
    hidden_l = jnp.concatenate([hidden_l, hidden_la])
    hidden_r = jnp.stack([hidden_r[0], hidden_rb[0], hidden_r[1], hidden_rb[1]])
    hidden_l = jnp.concatenate([hidden_l, swap(hidden_l, "core")]).reshape(8 * tokens, half)
    hidden_r = jnp.concatenate([hidden_r, swap(hidden_r, "core")]).reshape(8 * tokens, half)

    grad_o = [near_o[0], far_o[0], near_o[1], far_o[1], near_oa[0], far_oa[0], near_oa[1], far_oa[1]]
    grad_t = [near_t[0], far_t[0], near_tb[0], far_tb[0], near_t[1], far_t[1], near_tb[1], far_tb[1]]
    grad_other = jnp.stack(grad_o, 1).reshape(8 * tokens, own_rows)
    grad_own = jnp.stack(grad_t, 1).reshape(8 * tokens, own_rows)
    grad_other, grad_own, hidden_l, hidden_r, other_top, other_low = lax.optimization_barrier(
        (grad_other, grad_own, hidden_l, hidden_r, other_top, other_low)
    )

    grad_both = jnp.concatenate([grad_own, grad_other], 1)
    weights = jnp.concatenate([weight, other_top, other_low])
    w_l, w_r = weights[:, :half], weights[:, half:]
    edge = 4 * tokens
    away_l = inner(grad_both[edge:], w_l).astype(BF16)
    away_r = inner(after(grad_both, away_l)[edge:], w_r).astype(BF16)
    back_l, back_r = swap(away_l, "core"), swap(away_r, "core")
    sent_l = outer(after(grad_other, away_r), hidden_l).astype(BF16)
    got_l = swap(sent_l, "zl")
    back_l = after(back_l, sent_l)
    part_l = inner(grad_both[:edge], w_l) + back_l.astype(F32)
    part_l = part_l.reshape(2, 2, tokens, half)
    next_l = swap(part_l[1].astype(BF16), "y", "a")
    back_r = after(back_r, part_l)
    part_r = inner(grad_both[:edge], w_r) + back_r.astype(F32)
    part_r = part_r.reshape(2, 2, tokens, half)
    next_r = swap(part_r[:, 1].astype(BF16), "y", "b")
    sent_r = outer(after(grad_other, part_r), hidden_r).astype(BF16)
    got_r = swap(sent_r, "zl")
    next_l, next_r, got_l, sent_r = lax.optimization_barrier((next_l, next_r, got_l, sent_r))
    give_l = (part_l[0, 1] + next_l[1].astype(F32)).astype(BF16)
    give_r = (part_r[1, 0] + next_r[1].astype(F32)).astype(BF16)
    far_l, far_r = swap(give_l, "y", "b"), swap(give_r, "y", "a")
    kept_l = outer(after(grad_own, give_l, give_r), hidden_l)
    kept_r = outer(after(grad_own, kept_l), hidden_r)
    own_l = part_l[0, 0] + next_l[0].astype(F32)
    own_r = part_r[0, 0] + next_r[0].astype(F32)
    kept_l, kept_r, far_l, far_r = lax.optimization_barrier((kept_l, kept_r, far_l, far_r))
    grad_pre = finish(slope_l, slope_r, own_l, own_r, far_l, far_r)
    kept_l = (kept_l + got_l.astype(F32)).astype(BF16)
    kept_r = (kept_r + after(got_r, grad_pre).astype(F32)).astype(BF16)
    return (grad_pre, jnp.concatenate([kept_l, kept_r], 1))


def solution(mesh):
    sizes = tuple(SIZES[name] for name in NAMES)
    inner_mesh = Mesh(mesh.devices.reshape(sizes), NAMES)
    col, row = ("y", "zl", "core"), ("x", "zh")
    in_specs = (P(col, row, None), P(col, row), P(col, row))
    out_specs = (P(col, row), P(col, row))
    return jax.shard_map(shards, mesh=inner_mesh, in_specs=in_specs, out_specs=out_specs, check_vma=False)
```

```python
import functools
import math

import jax
import jax.numpy as jnp
from jax import lax
from jax.experimental import pallas as pl
from jax.experimental.pallas import tpu as pltpu
from jax.sharding import Mesh, PartitionSpec as P

NAMES = ("x", "zh", "y", "zl", "core")
SIZES = {"x": 4, "zh": 2, "y": 4, "zl": 2, "core": 2}
BF16, F32 = jnp.bfloat16, jnp.float32
VMEM = pl.BlockSpec(memory_space=pltpu.VMEM)
SMALL = pltpu.CompilerParams(vmem_limit_bytes=16 * 1024 * 1024)

STEP = {"b": lambda i: i ^ 1, "a": lambda i: 3 - i, "ab": lambda i: i ^ 2}


def swap(value, axis, step=None):
    move = STEP[step] if step else lambda i: 1 - i
    return lax.ppermute(value, axis, [(i, move(i)) for i in range(SIZES[axis])])


def around(axis):
    at = lax.axis_index(axis)
    return [at, at ^ 1, 3 - at, at ^ 2]


def after(value, *others):
    return lax.optimization_barrier((value,) + others)[0]


def gelu_parts(pre_float):
    cumulative = 0.5 * (1.0 + jax.scipy.special.erf(pre_float / math.sqrt(2.0)))
    density = jnp.exp(-0.5 * pre_float * pre_float) / math.sqrt(2.0 * math.pi)
    return (pre_float * cumulative, cumulative + pre_float * density)


def split_kernel(grad, near, away):
    size = near.shape[2] // 2
    zl, core = lax.axis_index("zl"), lax.axis_index("core")
    for out, k in ((near, core), (away, 1 - core)):
        for n, y in enumerate(around("y")):
            for z, other in enumerate((zl, 1 - zl)):
                at = pl.multiple_of(((y * 2 + other) * 2 + k) * size, size)
                out[n, :, z * size : (z + 1) * size] = grad[:, pl.ds(at, size)]


def split_grad(grad):
    rows, width = grad.shape
    piece = jax.ShapeDtypeStruct((4, rows, width // 8), BF16)
    return pl.pallas_call(split_kernel, in_specs=[VMEM], out_specs=[VMEM] * 2, out_shape=[piece, piece], compiler_params=SMALL)(grad)


def token_blocks(rows):
    zh = lax.axis_index("zh")
    return [pl.multiple_of((x * 2 + z) * rows, rows) for x in around("x") for z in (zh, 1 - zh)]


def hidden_kernel(pre, left, right, slope_l, slope_r):
    rows, half = pre.shape[0] // 8, pre.shape[1] // 2
    for n, at in enumerate(token_blocks(rows)):
        value, slope = gelu_parts(pre[pl.ds(at, rows), :].astype(F32))
        here = pl.ds(n * rows, rows)
        left[here, :] = value[:, :half].astype(BF16)
        right[here, :] = value[:, half:].astype(BF16)
        slope_l[here, :] = slope[:, :half]
        slope_r[here, :] = slope[:, half:]


def make_hidden(pre):
    tokens, units = pre.shape
    out = [jax.ShapeDtypeStruct((tokens, units // 2), t) for t in (BF16, BF16, F32, F32)]
    return pl.pallas_call(hidden_kernel, in_specs=[VMEM], out_specs=[VMEM] * 4, out_shape=out, compiler_params=SMALL)(pre)


def finish_kernel(slope_l, slope_r, own_l, own_r, far_l, far_r, out):
    rows, half = out.shape[0] // 8, out.shape[1] // 2
    for n, at in enumerate(token_blocks(rows)):
        here = pl.ds(n * rows, rows)
        left = (own_l[here, :] + far_l[here, :].astype(F32)) * slope_l[here, :]
        right = (own_r[here, :] + far_r[here, :].astype(F32)) * slope_r[here, :]
        out[pl.ds(at, rows), :half] = left.astype(BF16)
        out[pl.ds(at, rows), half:] = right.astype(BF16)


def finish(*args):
    tokens, half = args[0].shape
    out = jax.ShapeDtypeStruct((tokens, 2 * half), BF16)
    return pl.pallas_call(finish_kernel, in_specs=[VMEM] * 6, out_specs=VMEM, out_shape=out, compiler_params=SMALL)(*args)


def outer(g, h):
    return lax.dot_general(g, h, (((0,), (0,)), ((), ())), preferred_element_type=F32)


def inner(g, w):
    return jnp.dot(g, w, preferred_element_type=F32)


def shards(grad_out, pre_act, weight):
    rows, width = grad_out.shape[1:]
    tokens, units = pre_act.shape
    half = units // 2
    own_rows = weight.shape[0]

    near, away = split_grad(grad_out[0])
    sibling = swap(away, "core")
    cut = own_rows * 5 // 16
    other_top = swap(weight[:cut], "zl")

    both = jnp.stack([near, sibling])
    hidden_l, hidden_r, slope_l, slope_r = make_hidden(after(pre_act, both))
    grad = jnp.stack([both[:, 0]] + [swap(both[:, s], "y", m) for s, m in ((1, "b"), (2, "a"), (3, "ab"))], 1)
    grad = grad.reshape(8, rows, 2 * own_rows)

    near_o, near_t = grad[..., own_rows:], grad[..., :own_rows]
    near_ob, near_ta = swap(near_o, "x", "b"), swap(near_t, "x", "a")
    grad_far = swap(after(grad, other_top), "zh")
    hidden_l, hidden_r = after(hidden_l, grad), after(hidden_r, grad)
    hidden_lb, hidden_ra = swap(hidden_l, "y", "b"), swap(hidden_r, "y", "a")
    near_ob, near_ta = lax.optimization_barrier((near_ob, near_ta))
    near_o, near_t = jnp.stack([near_o, near_ob]), jnp.stack([near_t, near_ta])
    near_oa, near_tb = swap(near_o, "x", "a"), swap(near_t, "x", "b")
    hidden_l, hidden_r = jnp.stack([hidden_l, hidden_lb]), jnp.stack([hidden_r, hidden_ra])
    hidden_la, hidden_rb = swap(hidden_l, "y", "a"), swap(hidden_r, "y", "b")
    other_low = swap(after(weight[cut:], grad_far), "zl")
    near_oa, near_tb, grad_far = lax.optimization_barrier((near_oa, near_tb, grad_far))
    far_o, far_t = grad_far[..., own_rows:], grad_far[..., :own_rows]
    far_ob, far_ta = swap(far_o, "x", "b"), swap(far_t, "x", "a")
    far_ob, far_ta = lax.optimization_barrier((far_ob, far_ta))
    far_o, far_t = jnp.stack([far_o, far_ob]), jnp.stack([far_t, far_ta])
    far_oa, far_tb = swap(far_o, "x", "a"), swap(far_t, "x", "b")
    hidden_l = jnp.concatenate([hidden_l, hidden_la])
    hidden_r = jnp.stack([hidden_r[0], hidden_rb[0], hidden_r[1], hidden_rb[1]])
    hidden_l = jnp.concatenate([hidden_l, swap(hidden_l, "core")]).reshape(8 * tokens, half)
    hidden_r = jnp.concatenate([hidden_r, swap(hidden_r, "core")]).reshape(8 * tokens, half)

    grad_o = [near_o[0], far_o[0], near_o[1], far_o[1], near_oa[0], far_oa[0], near_oa[1], far_oa[1]]
    grad_t = [near_t[0], far_t[0], near_tb[0], far_tb[0], near_t[1], far_t[1], near_tb[1], far_tb[1]]
    grad_other = jnp.stack(grad_o, 1).reshape(8 * tokens, own_rows)
    grad_own = jnp.stack(grad_t, 1).reshape(8 * tokens, own_rows)
    grad_other, grad_own, hidden_l = lax.optimization_barrier((grad_other, grad_own, hidden_l))

    grad_both = jnp.concatenate([grad_own, grad_other], 1).reshape(2, 2, 2, tokens, 2 * own_rows)
    flat, pair = (2 * tokens, 2 * own_rows), (2, tokens, half)
    sent_l = outer(grad_other, hidden_l).astype(BF16)
    got_l = swap(sent_l, "zl")
    weights = jnp.concatenate([weight, other_top, after(other_low, sent_l)])
    w_l, w_r = weights[:, :half], weights[:, half:]
    away_l1 = inner(after(grad_both, sent_l)[1, 1].reshape(flat), w_l).astype(BF16)
    away_r1 = inner(after(grad_both, away_l1)[1, :, 1].reshape(flat), w_r).astype(BF16)
    back_1 = swap(jnp.stack([away_l1, away_r1]), "core")
    back_l1, back_r1 = back_1[0], back_1[1]
    part_l1 = inner(grad_both[0, 1].reshape(flat), w_l) + after(back_l1, away_r1).astype(F32)
    part_l1 = part_l1.astype(BF16)
    next_l = swap(part_l1.reshape(pair), "y", "a")
    part_r1 = inner(grad_both[0, :, 1].reshape(flat), w_r) + after(back_r1, part_l1).astype(F32)
    part_r1 = part_r1.astype(BF16)
    next_r = swap(part_r1.reshape(pair), "y", "b")
    tick_2 = swap(part_r1[:16, :128], "core")
    away_l0 = inner(after(grad_both, tick_2)[1, 0].reshape(flat), w_l).astype(BF16)
    away_r0 = inner(after(grad_both, away_l0)[1, :, 0].reshape(flat), w_r).astype(BF16)
    back_0 = swap(jnp.stack([away_l0, away_r0]), "core")
    sent_r = outer(after(grad_other, away_r0), hidden_r).astype(BF16)
    got_r = swap(sent_r, "zl")
    back_0 = after(back_0, sent_r)
    part_l0 = (inner(grad_both[0, 0].reshape(flat), w_l) + back_0[0].astype(F32)).reshape(pair)
    part_r0 = (inner(after(grad_both, part_l0)[0, :, 0].reshape(flat), w_r) + back_0[1].astype(F32)).reshape(pair)
    next_l, next_r, got_l, part_l0, part_r0 = lax.optimization_barrier((next_l, next_r, got_l, part_l0, part_r0))
    give_l = (part_l0[1] + next_l[1].astype(F32)).astype(BF16)
    give_r = (part_r0[1] + next_r[1].astype(F32)).astype(BF16)
    far_l, far_r = swap(give_l, "y", "b"), swap(give_r, "y", "a")
    kept_l = outer(after(grad_own, give_l, give_r), hidden_l)
    kept_r = outer(after(grad_own, kept_l), hidden_r)
    own_l = part_l0[0] + next_l[0].astype(F32)
    own_r = part_r0[0] + next_r[0].astype(F32)
    kept_l, kept_r = lax.optimization_barrier((kept_l, kept_r))
    kept_l = (kept_l + got_l.astype(F32)).astype(BF16)
    kept_r = (kept_r + got_r.astype(F32)).astype(BF16)
    kept = jnp.concatenate([kept_l, kept_r], 1)
    far_l, far_r, kept = lax.optimization_barrier((far_l, far_r, kept))
    grad_pre = finish(slope_l, slope_r, own_l, own_r, far_l, far_r)
    return (grad_pre, kept)


def solution(mesh):
    sizes = tuple(SIZES[name] for name in NAMES)
    inner_mesh = Mesh(mesh.devices.reshape(sizes), NAMES)
    col, row = ("y", "zl", "core"), ("x", "zh")
    in_specs = (P(col, row, None), P(col, row), P(col, row))
    out_specs = (P(col, row), P(col, row))
    return jax.shard_map(shards, mesh=inner_mesh, in_specs=in_specs, out_specs=out_specs, check_vma=False)
```

```python
import functools
import math

import jax
import jax.numpy as jnp
from jax import lax
from jax.experimental import pallas as pl
from jax.experimental.pallas import tpu as pltpu
from jax.sharding import Mesh, PartitionSpec as P

NAMES = ("x", "zh", "y", "zl", "core")
SIZES = {"x": 4, "zh": 2, "y": 4, "zl": 2, "core": 2}
BF16, F32 = jnp.bfloat16, jnp.float32
VMEM = pl.BlockSpec(memory_space=pltpu.VMEM)
SMALL = pltpu.CompilerParams(vmem_limit_bytes=24 * 1024 * 1024)

STEP = {"b": lambda i: i ^ 1, "a": lambda i: 3 - i, "ab": lambda i: i ^ 2}


def swap(value, axis, step=None):
    move = STEP[step] if step else lambda i: 1 - i
    return lax.ppermute(value, axis, [(i, move(i)) for i in range(SIZES[axis])])


def around(axis):
    at = lax.axis_index(axis)
    return [at, at ^ 1, 3 - at, at ^ 2]


def after(value, *others):
    return lax.optimization_barrier((value,) + others)[0]


def gelu_parts(pre_float):
    cumulative = 0.5 * (1.0 + jax.scipy.special.erf(pre_float / math.sqrt(2.0)))
    density = jnp.exp(-0.5 * pre_float * pre_float) / math.sqrt(2.0 * math.pi)
    return (pre_float * cumulative, cumulative + pre_float * density)


def split_kernel(grad, near, away):
    size = near.shape[2] // 2
    zl, core = lax.axis_index("zl"), lax.axis_index("core")
    for out, k in ((near, core), (away, 1 - core)):
        for n, y in enumerate(around("y")):
            for z, other in enumerate((zl, 1 - zl)):
                at = pl.multiple_of(((y * 2 + other) * 2 + k) * size, size)
                out[n, :, z * size : (z + 1) * size] = grad[:, pl.ds(at, size)]


def split_grad(grad):
    rows, width = grad.shape
    piece = jax.ShapeDtypeStruct((4, rows, width // 8), BF16)
    return pl.pallas_call(split_kernel, in_specs=[VMEM], out_specs=[VMEM] * 2, out_shape=[piece, piece], compiler_params=SMALL)(grad)


def token_blocks(rows):
    zh = lax.axis_index("zh")
    return [pl.multiple_of((x * 2 + z) * rows, rows) for x in around("x") for z in (zh, 1 - zh)]


def hidden_kernel(pre, left, right, slope_l, slope_r):
    rows, half = pre.shape[0] // 8, pre.shape[1] // 2
    for n, at in enumerate(token_blocks(rows)):
        value, slope = gelu_parts(pre[pl.ds(at, rows), :].astype(F32))
        here = pl.ds(n * rows, rows)
        left[here, :] = value[:, :half].astype(BF16)
        right[here, :] = value[:, half:].astype(BF16)
        slope_l[here, :] = slope[:, :half]
        slope_r[here, :] = slope[:, half:]


def make_hidden(pre):
    tokens, units = pre.shape
    out = [jax.ShapeDtypeStruct((tokens, units // 2), t) for t in (BF16, BF16, F32, F32)]
    return pl.pallas_call(hidden_kernel, in_specs=[VMEM], out_specs=[VMEM] * 4, out_shape=out, compiler_params=SMALL)(pre)


def finish_kernel(slope_l, slope_r, own_l, own_r, far_l, far_r, out):
    rows, half = out.shape[0] // 8, out.shape[1] // 2
    for n, at in enumerate(token_blocks(rows)):
        here = pl.ds(n * rows, rows)
        left = (own_l[here, :] + far_l[here, :].astype(F32)) * slope_l[here, :]
        right = (own_r[here, :] + far_r[here, :].astype(F32)) * slope_r[here, :]
        out[pl.ds(at, rows), :half] = left.astype(BF16)
        out[pl.ds(at, rows), half:] = right.astype(BF16)


def finish(*args):
    tokens, half = args[0].shape
    out = jax.ShapeDtypeStruct((tokens, 2 * half), BF16)
    return pl.pallas_call(finish_kernel, in_specs=[VMEM] * 6, out_specs=VMEM, out_shape=out, compiler_params=SMALL)(*args)


def outer(g, h):
    return lax.dot_general(g, h, (((0,), (0,)), ((), ())), preferred_element_type=F32)


def inner(g, w):
    return jnp.dot(g, w, preferred_element_type=F32)


def shards(grad_out, pre_act, weight):
    rows, width = grad_out.shape[1:]
    tokens, units = pre_act.shape
    half = units // 2
    own_rows = weight.shape[0]

    near, away = split_grad(grad_out[0])
    sibling = swap(away, "core")
    cut = own_rows * 5 // 16
    other_top = swap(weight[:cut], "zl")

    both = jnp.stack([near, sibling])
    hidden_l, hidden_r, slope_l, slope_r = make_hidden(after(pre_act, both))
    grad = jnp.stack([both[:, 0]] + [swap(both[:, s], "y", m) for s, m in ((1, "b"), (2, "a"), (3, "ab"))], 1)
    grad = grad.reshape(8, rows, 2 * own_rows)

    near_o, near_t = grad[..., own_rows:], grad[..., :own_rows]
    near_ob, near_ta = swap(near_o, "x", "b"), swap(near_t, "x", "a")
    grad_far = swap(after(grad, other_top), "zh")
    hidden_l, hidden_r = after(hidden_l, grad), after(hidden_r, grad)
    hidden_lb, hidden_ra = swap(hidden_l, "y", "b"), swap(hidden_r, "y", "a")
    near_ob, near_ta = lax.optimization_barrier((near_ob, near_ta))
    near_o, near_t = jnp.stack([near_o, near_ob]), jnp.stack([near_t, near_ta])
    near_oa, near_tb = swap(near_o, "x", "a"), swap(near_t, "x", "b")
    hidden_l, hidden_r = jnp.stack([hidden_l, hidden_lb]), jnp.stack([hidden_r, hidden_ra])
    hidden_la, hidden_rb = swap(hidden_l, "y", "a"), swap(hidden_r, "y", "b")
    other_low = swap(after(weight[cut:], grad_far), "zl")
    near_oa, near_tb, grad_far = lax.optimization_barrier((near_oa, near_tb, grad_far))
    far_o, far_t = grad_far[..., own_rows:], grad_far[..., :own_rows]
    far_ob, far_ta = swap(far_o, "x", "b"), swap(far_t, "x", "a")
    far_ob, far_ta = lax.optimization_barrier((far_ob, far_ta))
    far_o, far_t = jnp.stack([far_o, far_ob]), jnp.stack([far_t, far_ta])
    far_oa, far_tb = swap(far_o, "x", "a"), swap(far_t, "x", "b")
    hidden_l = jnp.concatenate([hidden_l, hidden_la])
    hidden_r = jnp.stack([hidden_r[0], hidden_rb[0], hidden_r[1], hidden_rb[1]])
    hidden_l = jnp.concatenate([hidden_l, swap(hidden_l, "core")]).reshape(8 * tokens, half)
    hidden_r = jnp.concatenate([hidden_r, swap(hidden_r, "core")]).reshape(8 * tokens, half)

    grad_o = [near_o[0], far_o[0], near_o[1], far_o[1], near_oa[0], far_oa[0], near_oa[1], far_oa[1]]
    grad_t = [near_t[0], far_t[0], near_tb[0], far_tb[0], near_t[1], far_t[1], near_tb[1], far_tb[1]]
    grad_other = jnp.stack(grad_o, 1).reshape(8 * tokens, own_rows)
    grad_own = jnp.stack(grad_t, 1).reshape(8 * tokens, own_rows)
    grad_other, grad_own, hidden_l = lax.optimization_barrier((grad_other, grad_own, hidden_l))

    grad_both = jnp.concatenate([grad_own, grad_other], 1).reshape(2, 2, 2, tokens, 2 * own_rows)
    flat, pair = (2 * tokens, 2 * own_rows), (2, tokens, half)
    sent_l = outer(grad_other, hidden_l).astype(BF16)
    got_l = swap(sent_l, "zl")
    weights = jnp.concatenate([weight, other_top, after(other_low, sent_l)])
    w_l, w_r = weights[:, :half], weights[:, half:]
    away_l1 = inner(after(grad_both, sent_l)[1, 1].reshape(flat), w_l).astype(BF16)
    away_r1 = inner(after(grad_both, away_l1)[1, :, 1].reshape(flat), w_r).astype(BF16)
    back_1 = swap(jnp.stack([away_l1, away_r1]), "core")
    back_l1, back_r1 = back_1[0], back_1[1]
    part_l1 = inner(grad_both[0, 1].reshape(flat), w_l) + after(back_l1, away_r1).astype(F32)
    part_l1 = part_l1.astype(BF16)
    next_l = swap(part_l1.reshape(pair), "y", "a")
    part_r1 = inner(grad_both[0, :, 1].reshape(flat), w_r) + after(back_r1, part_l1).astype(F32)
    part_r1 = part_r1.astype(BF16)
    next_r = swap(part_r1.reshape(pair), "y", "b")
    tick_2 = swap(part_r1[:16, :128], "core")
    away_l0 = inner(after(grad_both, tick_2)[1, 0].reshape(flat), w_l).astype(BF16)
    away_r0 = inner(after(grad_both, away_l0)[1, :, 0].reshape(flat), w_r).astype(BF16)
    back_0 = swap(jnp.stack([away_l0, away_r0]), "core")
    sent_r = outer(after(grad_other, away_r0), hidden_r).astype(BF16)
    got_r = swap(sent_r, "zl")
    back_0 = after(back_0, sent_r)
    part_l0 = (inner(grad_both[0, 0].reshape(flat), w_l) + back_0[0].astype(F32)).reshape(pair)
    part_r0 = (inner(after(grad_both, part_l0)[0, :, 0].reshape(flat), w_r) + back_0[1].astype(F32)).reshape(pair)
    next_l, next_r, got_l, part_l0, part_r0 = lax.optimization_barrier((next_l, next_r, got_l, part_l0, part_r0))
    give_l = (part_l0[1] + next_l[1].astype(F32)).astype(BF16)
    give_r = (part_r0[1] + next_r[1].astype(F32)).astype(BF16)
    far_l, far_r = swap(give_l, "y", "b"), swap(give_r, "y", "a")
    kept_l = outer(after(grad_own, give_l, give_r), hidden_l)
    kept_r = outer(after(grad_own, kept_l), hidden_r)
    own_l = part_l0[0] + next_l[0].astype(F32)
    own_r = part_r0[0] + next_r[0].astype(F32)
    kept_l, kept_r = lax.optimization_barrier((kept_l, kept_r))
    kept_l = (kept_l + got_l.astype(F32)).astype(BF16)
    kept_r = (kept_r + got_r.astype(F32)).astype(BF16)
    kept = jnp.concatenate([kept_l, kept_r], 1)
    far_l, far_r, kept = lax.optimization_barrier((far_l, far_r, kept))
    grad_pre = finish(slope_l, slope_r, own_l, own_r, far_l, far_r)
    return (grad_pre, kept)


def solution(mesh):
    sizes = tuple(SIZES[name] for name in NAMES)
    inner_mesh = Mesh(mesh.devices.reshape(sizes), NAMES)
    col, row = ("y", "zl", "core"), ("x", "zh")
    in_specs = (P(col, row, None), P(col, row), P(col, row))
    out_specs = (P(col, row), P(col, row))
    return jax.shard_map(shards, mesh=inner_mesh, in_specs=in_specs, out_specs=out_specs, check_vma=False)
```
